32 devices in a mesh: dp: 8 (over z, x), mp: 4 (over y, core).
Axes of the slice: x: 2, y: 2, z: 4, core: 2. Of those that a mesh axis runs over, the one named last changes fastest.
Arguments:
- hidden_in: bfloat16 [16384, 768], P(('dp', 'mp')), may hold values from -6 to 6
- box_coords: int32 [16384, 4], P(('dp', 'mp')), may hold values from 0 to 999
- page_lengths: int32 [32, 6], P('dp'), may hold values from 1 to 400, 480 in all within a row
- qkv_weight: bfloat16 [768, 3, 768], P(None, None, 'mp'), may hold values from -0.21875 to 0.21875
- box_weight: bfloat16 [128, 768], P(None, 'mp'), may hold values from -0.75 to 0.75
- out_weight: bfloat16 [768, 768], P('mp'), may hold values from -0.875 to 0.875
- norm1_gain: float32 [768], replicated, may hold values from 0.5 to 1.5
- norm1_bias: float32 [768], replicated, may hold values from -1 to 1
- up_weight: bfloat16 [768, 3072], P(None, 'mp'), may hold values from -0.21875 to 0.21875
- up_bias: bfloat16 [3072], P('mp'), may hold values from -1.5 to 1.5
- down_weight: bfloat16 [3072, 768], P('mp'), may hold values from -0.15625 to 0.15625
- norm2_gain: float32 [768], replicated, may hold values from 0.5 to 1.5
- norm2_bias: float32 [768], replicated, may hold values from -1 to 1
- out_grad: bfloat16 [16384, 768], P(('dp', 'mp')), may hold values from -6 to 6
Outputs:
- layer_out: bfloat16 [16384, 768], P(('dp', 'mp'))
- input_grad: float32 [16384, 768], P(('dp', 'mp'))
- qkv_weight_grad: float32 [768, 3, 768], P(None, None, 'mp')
- box_weight_grad: float32 [128, 768], P(None, 'mp')
- out_weight_grad: float32 [768, 768], P('mp')
- norm1_gain_grad: float32 [768], replicated
- norm1_bias_grad: float32 [768], replicated
- up_weight_grad: float32 [768, 3072], P(None, 'mp')
- up_bias_grad: float32 [3072], P('mp')
- down_weight_grad: float32 [3072, 768], P('mp')
- norm2_gain_grad: float32 [768], replicated
- norm2_bias_grad: float32 [768], replicated
The draws below stay inside these ranges and needn't reach their ends.
Inputs may be any that keep to these rules, and one draw needn't show every extreme that they name: `page_lengths`: each slot's 6 lengths sum to 480; the slot's remaining positions are padding.
All inputs are finite; a program needn't handle non-finite values.
Results may differ from the reference program's by a relative error of at most 0.015.
The reference program's roundings to bfloat16 on the way count: a program that leaves them out, or rounds other values in their place, can miss the bound.
Values may be sent and summed in bfloat16 or wider, within the bound.
A program may use at most 128 MiB of HBM per device.

```python
import math
import jax
import jax.numpy as jnp
import numpy as np
from jax import lax

D = 768
HEADS = 12
HEAD_DIM = 64
FF = 3072
BOX_DIM = 128
SLOT_LEN = 512
PAGES_SLOT = 6
SLOTS_DEV = 4
FILLED = 480
PAGE_MOST = 400
SLOTS = 32
TOKENS = 16384
N_DP = 8


def plant(array, rng, low, top_value):
    longest = array.shape.index(max(array.shape))
    spots = []
    for shift in (0, 1):
        where = [jax.random.randint(jax.random.fold_in(rng, axis), (), 0, length) for axis, length in enumerate(array.shape)]
        where[longest] = (where[longest] + shift) % array.shape[longest]
        spots.append(tuple(where))
    return array.at[spots[0]].set(low).at[spots[1]].set(top_value)


def block_levels(stream_key, dims, cuts, smallest, top_value):
    loudness = 1.0
    for dim, parts in cuts:
        draws = jax.random.uniform(jax.random.fold_in(jax.random.fold_in(stream_key, 6), dim), (parts,), jnp.float32, smallest / len(cuts), top_value / len(cuts))
        loudness = loudness * jnp.repeat(jnp.exp(draws), dims[dim] // parts).reshape((-1,) + (1,) * (len(dims) - 1 - dim))
    return loudness


def split_up(number_of, total, most, skew):
    loads = [(1 << 20) // math.isqrt(rank ** skew) + 1 for rank in range(2, number_of + 1)]
    surplus, counts = total - most - (number_of - 1), [1] * (number_of - 1)
    while surplus > 0:
        movable = [i for i in range(number_of - 1) if counts[i] < most]
        mass, budget = sum([loads[i] for i in movable]), surplus
        for i in movable:
            extra = min(most - counts[i], max(1, budget * loads[i] // mass), surplus)
            counts[i] = counts[i] + extra
            surplus = surplus - extra
    return np.array([most] + counts)


def ragged(key, count, total, most, lean):
    if count == 2:
        one = jax.random.randint(key, (), max(1, total - most), min(most, total - 1) + 1)
        return jnp.stack([one, total - one])
    tallies = jnp.asarray(split_up(count, total, most, lean), jnp.int32)
    pairs = (count - 1) // 2
    donor, taker = tallies[1:1 + 2 * pairs:2], tallies[2:2 + 2 * pairs:2]
    room = jnp.minimum(donor - 1, most - taker)
    passed = jax.random.randint(jax.random.fold_in(key, 1), (pairs,), 0, 1 << 20) % (room + 1)
    tallies = tallies.at[1:1 + 2 * pairs:2].set(donor - passed).at[2:2 + 2 * pairs:2].set(taker + passed)
    return tallies[jax.random.permutation(jax.random.fold_in(key, 2), count)]


def noise(key, dims, spread, most, pieces=(), kind=jnp.bfloat16):
    gain = block_levels(key, dims, pieces, -0.22, 0.18) if pieces else 1.0
    array = jax.random.normal(key, dims, jnp.float32) * spread * gain
    return jnp.minimum(jnp.maximum(array, -most), most).astype(kind)


def setup_inputs(seed: int = 0) -> dict:
    seeds = jax.random.split(jax.random.key(seed), 15)
    return {
        "hidden_in": noise(seeds[0], (TOKENS, D), 1.0, 6.0, ((0, 32),)),
        "box_coords": plant(jax.random.randint(seeds[1], (TOKENS, 4), 0, 1000), jax.random.fold_in(seeds[1], 1), 0, 999).astype(jnp.int32),
        "page_lengths": jax.vmap(lambda own: ragged(own, PAGES_SLOT, FILLED, PAGE_MOST, 2))(jax.random.split(seeds[2], SLOTS)).reshape((SLOTS, PAGES_SLOT)).astype(jnp.int32),
        "qkv_weight": noise(seeds[3], (D, 3, D), D ** -0.5, 0.21875, ((2, 4),)),
        "box_weight": noise(seeds[4], (BOX_DIM, D), HEAD_DIM ** -0.5, 0.75, ((1, 4),)),
        "out_weight": noise(seeds[5], (D, D), (D // 16) ** -0.5, 0.875, ((0, 4),)),
        "norm1_gain": jnp.clip(1.0 + 0.1 * jax.random.normal(seeds[6], (D,), jnp.float32), 0.5, 1.5),
        "norm1_bias": noise(seeds[7], (D,), 0.2, 1.0, (), jnp.float32),
        "up_weight": noise(seeds[8], (D, FF), D ** -0.5, 0.21875, ((1, 4),)),
        "up_bias": noise(seeds[9], (FF,), 0.3, 1.5, ((0, 4),)),
        "down_weight": noise(seeds[10], (FF, D), (FF // 2) ** -0.5, 0.15625, ((0, 4),)),
        "norm2_gain": jnp.clip(1.0 + 0.1 * jax.random.normal(seeds[11], (D,), jnp.float32), 0.5, 1.5),
        "norm2_bias": noise(seeds[12], (D,), 0.2, 1.0, (), jnp.float32),
        "out_grad": noise(seeds[13], (TOKENS, D), 1.0, 6.0, ((0, 32),)),
    }


@jax.custom_vjp
def low(v):
    return lax.optimization_barrier(v.astype(jnp.bfloat16)).astype(jnp.float32)

@jax.custom_vjp
def low_back(v):
    return v

def low_keep(v):
    return (low(v), None)

def low_pass(kept, grad):
    return (grad,)

def back_keep(v):
    return (v, None)

def back_low(kept, grad):
    return (low(grad),)
low.defvjp(low_keep, low_pass)
low_back.defvjp(back_keep, back_low)
PRECISE = lax.Precision.HIGHEST
EPSILON = 1e-05
MASKED = -1000000000.0

def box_features(box_coords, feat_width):
    freq_count = feat_width // 8
    frequency = jnp.exp(-jnp.log(10000.0) * jnp.arange(freq_count, dtype=jnp.float32) / freq_count)
    angles = box_coords.astype(jnp.float32)[:, :, None] * frequency[None, None, :]
    angles = angles.reshape(box_coords.shape[0], 4 * freq_count)
    return jnp.concatenate([jnp.cos(angles), jnp.sin(angles)], axis=1)

def segments(lengths):
    page_ends = jnp.cumsum(lengths).astype(jnp.int32)
    position = jnp.arange(SLOT_LEN, dtype=jnp.int32)
    return lax.optimization_barrier(jnp.sum((position[:, None] >= page_ends[None, :]).astype(jnp.int32), axis=1)).astype(jnp.int32)

def layer_norm(values, norm_gain, norm_bias):
    row_mean = lax.optimization_barrier(jnp.mean(values, axis=-1, keepdims=True))
    centred = values - row_mean
    variance = lax.optimization_barrier(jnp.mean(centred * centred, axis=-1, keepdims=True))
    return centred * lax.rsqrt(variance + EPSILON) * norm_gain + norm_bias

def gelu_exact(values):
    return 0.5 * values * (1.0 + lax.erf(values * 0.7071067811865476))

def slot_attention(inputs):
    query_block, key_block, value_block, id_block = inputs
    raw_scores = jnp.einsum('ihe,jhe->hij', query_block, key_block, precision=PRECISE) * HEAD_DIM ** (-0.5)
    same_page = id_block[:, None] == id_block[None, :]
    scores = low_back(jnp.where(same_page[None], raw_scores, MASKED))
    row_max = lax.optimization_barrier(jnp.max(scores, axis=-1, keepdims=True))
    exp_terms = jnp.exp(scores - row_max)
    probability = low(exp_terms / lax.optimization_barrier(jnp.sum(exp_terms, axis=-1, keepdims=True)))
    return jnp.einsum('hij,jhe->ihe', probability, value_block, precision=PRECISE)

def forward(hidden, features, page_ids, qkv_weight, box_weight, out_weight, norm1_gain, norm1_bias, up_weight, up_bias, down_weight, norm2_gain, norm2_bias):
    row_count = hidden.shape[0]
    projected = jnp.einsum('nd,dce->nce', hidden, qkv_weight, precision=PRECISE)
    queries = low_back(low(projected[:, 0])).reshape(row_count, HEADS, HEAD_DIM)
    key_rows = low_back(low(projected[:, 1])).reshape(row_count, HEADS, HEAD_DIM)
    value_rows = low_back(low(projected[:, 2])).reshape(row_count, HEADS, HEAD_DIM)
    half_width = BOX_DIM // 2
    box_heads = box_weight.reshape(BOX_DIM, HEADS, HEAD_DIM)
    box_turn = low_back(jnp.einsum('nhe,phe->nhp', queries, box_heads, precision=PRECISE))
    cosine = features[:, None, :half_width]
    sine_part = features[:, None, half_width:]
    sin_coef = box_turn[..., :half_width]
    cos_coef = box_turn[..., half_width:]
    rotated = low(jnp.concatenate([sin_coef * sine_part + cos_coef * cosine, cos_coef * sine_part - sin_coef * cosine], axis=-1))
    aug_width = HEAD_DIM + BOX_DIM
    query_aug = jnp.concatenate([queries, rotated], axis=-1).reshape(SLOTS_DEV, SLOT_LEN, HEADS, aug_width)
    key_aug = jnp.concatenate([key_rows, jnp.broadcast_to(features[:, None, :], (row_count, HEADS, BOX_DIM))], axis=-1).reshape(SLOTS_DEV, SLOT_LEN, HEADS, aug_width)
    value_slots = value_rows.reshape(SLOTS_DEV, SLOT_LEN, HEADS, HEAD_DIM)
    context = lax.map(jax.checkpoint(slot_attention), (query_aug, key_aug, value_slots, page_ids))
    context = low_back(low(context.reshape(row_count, HEADS * HEAD_DIM)))
    attended = low_back(jnp.dot(context, out_weight, precision=PRECISE))
    normed = layer_norm(hidden + attended, norm1_gain, norm1_bias)
    ffn_pre = low_back(jnp.dot(low(normed), up_weight, precision=PRECISE) + up_bias)
    active = low(gelu_exact(ffn_pre))
    branch = low_back(jnp.dot(active, down_weight, precision=PRECISE))
    return layer_norm(normed + branch, norm2_gain, norm2_bias)

def reference(hidden_in, box_coords, page_lengths, qkv_weight, box_weight, out_weight, norm1_gain, norm1_bias, up_weight, up_bias, down_weight, norm2_gain, norm2_bias, out_grad):
    weights = tuple((weight.astype(jnp.float32) for weight in (qkv_weight, box_weight, out_weight, norm1_gain, norm1_bias, up_weight, up_bias, down_weight, norm2_gain, norm2_bias)))
    group_rows = SLOTS_DEV * SLOT_LEN
    hidden_all = hidden_in.astype(jnp.float32).reshape(N_DP, group_rows, D)
    boxes_all = box_coords.reshape(N_DP, group_rows, 4)
    lengths_all = page_lengths.reshape(N_DP, SLOTS_DEV, PAGES_SLOT)
    grads_all = out_grad.astype(jnp.float32).reshape(N_DP, group_rows, D)

    def one_group(totals, inputs):
        hidden, box_group, lengths, cotangent = inputs
        features = low(box_features(box_group, BOX_DIM))
        page_ids = jax.vmap(segments)(lengths)

        def closed(hidden_rows, *params):
            return forward(hidden_rows, features, page_ids, *params)
        result, pullback = jax.vjp(closed, hidden, *weights)
        pulled = pullback(cotangent)
        totals = tuple((left + right for left, right in zip(totals, pulled[1:])))
        return (totals, (result.astype(jnp.bfloat16), pulled[0]))
    initial = tuple((jnp.zeros_like(weight) for weight in weights))
    totals, (layer_outs, input_grads) = lax.scan(one_group, initial, (hidden_all, boxes_all, lengths_all, grads_all))
    return (layer_outs.reshape(TOKENS, D), input_grads.reshape(TOKENS, D), totals[0], totals[1], totals[2], totals[3], totals[4], totals[5], totals[6], totals[7], totals[8], totals[9])
```

```python
import functools

import jax
import jax.numpy as jnp
from jax import lax
from jax.experimental import pallas as pl
from jax.experimental.pallas import tpu as pltpu
from jax.sharding import PartitionSpec as P

HEAD_DIM = 64
EPSILON = 1e-05
MASKED = -1000000000.0
ROOT_HALF = 0.7071067811865476
INV_ROOT_TAU = 0.3989422804014327
BF16 = jnp.bfloat16
F32 = jnp.float32


def mm(a, b):
    return jnp.dot(a, b, preferred_element_type=F32)


def mm_t(a, b):
    return lax.dot_general(a, b, (((1,), (1,)), ((), ())), preferred_element_type=F32)


def lanes(n):
    return pl.ds(pl.multiple_of(n, 128), 128)


def half_mask(h, dtype):
    lane = lax.broadcasted_iota(jnp.int32, (1, 128), 1)
    return jnp.where((lane < 64) == (h == 0), 1.0, 0.0).astype(dtype)


MESH = pl.DeviceIdType.MESH


class Wire:
    def __init__(self, send, recv):
        self.send, self.recv, self.count, self.sent = send, recv, 0, []

    def copy(self, src, dst, device):
        i = self.count
        self.count += 1
        made = pltpu.make_async_remote_copy(src_ref=src, dst_ref=dst, send_sem=self.send.at[i], recv_sem=self.recv.at[i],
                                            device_id=device, device_id_type=MESH)
        self.sent.append(made)
        return made

    def settle(self, made):
        made.wait_send()
        self.sent = [other for other in self.sent if other is not made]

    def drain(self):
        for made in self.sent:
            made.wait_send()


class Place:
    def __init__(self):
        dp, mp = lax.axis_index("dp"), lax.axis_index("mp")
        r = lax.rem(dp, 8)
        base = dp - r
        self.y, self.c = lax.div(mp, 2), lax.rem(mp, 2)
        self.z, self.x = lax.div(r, 2), lax.rem(r, 2)
        self.me = mp
        self.part = (dp, self.y * 2 + 1 - self.c)
        self.ynb = (dp, (1 - self.y) * 2 + self.c)
        self.xnb = (base + self.z * 2 + 1 - self.x, mp)
        self.zz = lax.rem(self.z, 2)
        self.znb = (base + (self.z + 1 - 2 * self.zz) * 2 + self.x, mp)
        self.zk = [lax.rem(self.z + k, 4) for k in (1, 2, 3)]
        self.zdev = [(base + k * 2 + self.x, mp) for k in self.zk]
        self.far_part = (1 - self.y) * 2 + 1 - self.c
        self.far_mine = (1 - self.y) * 2 + self.c
        self.near_part = self.y * 2 + 1 - self.c

    def greet(self):
        barrier = pltpu.get_barrier_semaphore()
        for device in [self.part, self.ynb, self.xnb] + self.zdev:
            pl.semaphore_signal(barrier, inc=1, device_id=device, device_id_type=MESH)
        pl.semaphore_wait(barrier, 6)


def rows_of(ref, start, size):
    return ref.at[pl.ds(pl.multiple_of(start, 16), size)]


class Gather:
    def __init__(self, wire, place, own, whole, size):
        self.place = place
        q = size // 4
        at_own = lambda k: own.at[pl.ds(pl.multiple_of(k * q, 16), q)]
        at = lambda j, k: whole(j).at[pl.ds(pl.multiple_of(k * q, 16), q)]

        def half(j, k, h):
            v = at(j, k)
            w = v.shape[-1] // 2
            return v.at[:, pl.ds(h * w, w)]

        x, zz, jy = place.x, place.zz, place.far_mine
        mine, qx, qz, qd = x + 2 * zz, 1 - x + 2 * zz, x + 2 * (1 - zz), 1 - x + 2 * (1 - zz)
        same = lambda v, dev: wire.copy(v, v, dev)
        self.own = wire.copy(own, whole(place.me), place.part)
        self.over = wire.copy(at_own(mine), at(place.me, mine), place.ynb)
        self.fx, self.fz, self.f0 = [same(at(jy, mine), d) for d in (place.xnb, place.znb, place.part)]
        self.dx, self.dz = same(half(jy, qz, 0), place.xnb), same(half(jy, qx, 1), place.znb)
        self.f1, self.f2, self.f3 = [same(at(jy, k), place.part) for k in (qx, qz, qd)]

    def g0(self):
        self.over.start()
        self.own.start()

    def g1(self):
        self.over.wait_recv()
        self.fx.start()
        self.fz.start()
        self.f0.start()

    def g2(self):
        self.fx.wait_recv()
        self.fz.wait_recv()
        self.dx.start()
        self.dz.start()
        self.f1.start()
        self.f2.start()

    def g3(self):
        self.dx.wait_recv()
        self.dz.wait_recv()
        self.f3.start()

    def near(self):
        self.own.wait_recv()

    def far(self):
        for made in (self.f0, self.f1, self.f2, self.f3):
            made.wait_recv()


class SmallGather:
    def __init__(self, wire, place, own, whole):
        self.own = wire.copy(own, whole(place.me), place.part)
        self.over = wire.copy(own, whole(place.me), place.ynb)
        jy = place.far_mine
        self.f0 = wire.copy(whole(jy), whole(jy), place.part)

    def g0(self):
        self.over.start()
        self.own.start()

    def g1(self):
        self.over.wait_recv()
        self.f0.start()

    def near(self):
        self.own.wait_recv()

    def far(self):
        self.f0.wait_recv()


def accumulate(dst, *srcs, out=None):
    rows, cols = dst.shape
    step = next(s for s in (256, 192, 128, 96, 64, 48, 32, 16) if rows % s == 0 and (s * cols <= 24576 or s == 16))

    def one(i, carry):
        rs = pl.ds(pl.multiple_of(i * step, 16), step)
        total = dst[rs, :].astype(F32)
        for s in srcs:
            total = total + s[rs, :].astype(F32)
        (dst if out is None else out)[rs, :] = total.astype(dst.dtype)
        return carry

    lax.fori_loop(0, rows // step, one, 0)


class Reduce:
    def __init__(self, wire, place, grad, rc, ry, rx, rz, split=True):
        self.wire, self.place, self.split = wire, place, split
        mine = grad(place.me)
        rows, cols = mine.shape
        r4, c2 = rows // 4, cols // 2 if split else cols
        cut = (lambda h: pl.ds(pl.multiple_of(h * c2, 128), c2)) if split else (lambda h: slice(None))
        half = lambda v, h: v.at[:, cut(h)]
        piece = lambda v, k: v.at[pl.ds(pl.multiple_of(k * r4, 16), r4), cut(place.x)]
        self.c0 = wire.copy(grad(place.far_part), rc(0), place.part)
        self.c1 = wire.copy(grad(place.near_part), rc(1), place.part)
        self.yc = wire.copy(grad(place.far_mine), ry, place.ynb)
        self.xc = wire.copy(half(mine, 1 - place.x), rx, place.xnb)
        self.zc = [wire.copy(piece(mine, place.zk[k]), rz(k), place.zdev[k]) for k in range(3)]
        own, done = piece(mine, place.z), piece(ry, place.z)
        self.az = [wire.copy(done, done, place.zdev[k]) for k in range(3)]
        mh, dh = half(mine, place.x), half(ry, place.x)
        self.ax = wire.copy(dh, dh, place.xnb) if split else None
        self.done = done
        self.far, self.mine, self.own, self.mh, self.rc, self.ry, self.rx, self.rz = grad(place.far_mine), mine, own, mh, rc, ry, rx, rz

    def s0a(self):
        self.c0.start()

    def s0b(self):
        self.c1.start()

    def s1(self):
        self.c0.wait_recv()
        accumulate(self.far, self.rc(0))
        self.yc.start()

    def s2(self):
        self.c1.wait_recv()
        self.yc.wait_recv()
        accumulate(self.mine, self.rc(1), self.ry)
        self.xc.start()

    def s3(self):
        self.xc.wait_recv()
        if not self.split:
            self.wire.settle(self.xc)
        accumulate(self.mh, self.rx)
        for made in self.zc:
            made.start()

    def s4(self):
        for made in self.zc:
            made.wait_recv()
        accumulate(self.own, *[self.rz(k) for k in range(3)], out=self.done)
        for made in self.az:
            made.start()

    def s5(self):
        for made in self.az:
            made.wait_recv()
        if self.split:
            self.ax.start()

    def s6(self):
        if self.split:
            self.ax.wait_recv()


class SmallReduce:
    def __init__(self, wire, place, grad, rc, ry, rx, rz):
        self.wire, self.place, self.grad, self.rc, self.ry, self.rx, self.rz = wire, place, grad, rc, ry, rx, rz
        self.c0 = wire.copy(grad.at[place.far_part], rc.at[0], place.part)
        self.c1 = wire.copy(grad.at[place.near_part], rc.at[1], place.part)
        self.yc = wire.copy(grad.at[place.far_mine], ry, place.ynb)
        self.xc = wire.copy(grad.at[place.me], rx, place.xnb)
        self.zc = [wire.copy(grad.at[place.me], rz.at[place.z], d) for d in place.zdev]

    def s0a(self):
        self.c0.start()

    def s0b(self):
        self.c1.start()

    def s1(self):
        self.c0.wait_recv()
        j = self.place.far_mine
        self.grad[j] = self.grad[j] + self.rc[0]
        self.yc.start()

    def s2(self):
        self.c1.wait_recv()
        self.yc.wait_recv()
        j = self.place.me
        self.grad[j] = (self.grad[j] + self.rc[1]) + self.ry[...]
        self.xc.start()

    def s3(self):
        self.xc.wait_recv()
        self.wire.settle(self.xc)
        j = self.place.me
        total = self.grad[j] + self.rx[...]
        self.grad[j] = total
        self.rz[self.place.z] = total
        for made in self.zc:
            made.start()

    def s4(self):
        for made in self.zc:
            made.wait_recv()
        for made in self.zc:
            self.wire.settle(made)
        self.grad[self.place.me] = (self.rz[0] + self.rz[1]) + (self.rz[2] + self.rz[3])

    def s5(self):
        pass

    def s6(self):
        pass


def low_half(a, b):
    lane = lax.broadcasted_iota(jnp.int32, a.shape, 1)
    return jnp.where(lane < 64, a, b)


N_COPY = 230


def kernel(x_in, coords, lengths, og_in, q_in, box_in, out_in, up_in, upb_in, dn_in, n1g, n1b, n2g, n2b,
           lo, ig, gq_out, gbox_out, gout_out, gup_out, gdn_out, small_out,
           x, wq, wbox, wout, wup, upb, wdn, gbox, gup, gdn, small,
           feat, sin2, cos2, mask, qp, kp, vp, prob, ctx, hat1, inv1, nl, nlt, actt, slp, br, bg, boxr, do,
           rc_up, rc_dn, ry_up, ry_dn, rx_up, rx_dn, rz_up, rz_dn, rc_q, ry_q, rx_q, rz_q, rc_o, ry_o, rx_o, rz_o,
           rc_b, ry_b, rx_b, rz_b, rc_s, ry_s, rx_s, rz_s, send, recv, local):
    rows, d = x.shape
    n_tile = wup.shape[0]
    loc = q_in.shape[1]
    place = Place()
    me, y = place.me, place.y
    wire = Wire(send, recv)
    near, far = y * 384, (1 - y) * 384

    gq = wup
    gout = wup.at[3]
    dt = actt

    gat_q = [Gather(wire, place, q_in.at[w], lambda j, w=w: wq.at[w, pl.ds(pl.multiple_of(j * loc, 16), loc)], loc) for w in range(3)]
    gat_o = Gather(wire, place, out_in, lambda j: wout.at[pl.ds(pl.multiple_of(j * loc, 16), loc)], loc)
    gat_u = Gather(wire, place, up_in, lambda j: wup.at[j], up_in.shape[0])
    gat_d = Gather(wire, place, dn_in, lambda j: wdn.at[j], dn_in.shape[0])
    gat_b = SmallGather(wire, place, box_in, lambda j: wbox.at[pl.ds(pl.multiple_of(j * loc, 16), loc)])
    gat_s = SmallGather(wire, place, upb_in, lambda j: upb.at[j])
    gathers = gat_q + [gat_b, gat_o, gat_s, gat_u, gat_d]

    ups, dns = [], []
    for s in range(3):
        cs = slice(s * 256, (s + 1) * 256)
        ups.append(Reduce(wire, place, lambda j, cs=cs: gup.at[j, :, cs], lambda i, cs=cs: rc_up.at[i, :, cs], ry_up.at[:, cs],
                          rx_up.at[s], lambda k, s=s: rz_up.at[s, k]))
        dns.append(Reduce(wire, place, lambda j, cs=cs: gdn.at[j, cs], lambda i, cs=cs: rc_dn.at[i, cs], ry_dn.at[cs],
                          rx_dn.at[s], lambda k, s=s: rz_dn.at[s, k]))
    qs = [Reduce(wire, place, lambda j, w=w: gq.at[w, pl.ds(pl.multiple_of(j * loc, 16), loc)], lambda i, w=w: rc_q.at[i, w], ry_q.at[w],
                 rx_q.at[w], lambda k, w=w: rz_q.at[w, k]) for w in range(3)]
    outr = Reduce(wire, place, lambda j: gout.at[pl.ds(pl.multiple_of(j * loc, 16), loc)], lambda i: rc_o.at[i], ry_o, rx_o, lambda k: rz_o.at[k])
    boxs = Reduce(wire, place, lambda j: gbox.at[pl.ds(pl.multiple_of(j * loc, 16), loc)], lambda i: rc_b.at[i], ry_b, rx_b,
                  lambda k: rz_b.at[k], split=False)
    smalls = SmallReduce(wire, place, small, rc_s, ry_s, rx_s, rz_s)
    assert wire.count <= N_COPY
    queue = [[ups[0]], [dns[0]], [ups[1]], [dns[1]], [ups[2]], [dns[2]], [outr, smalls], [qs[0], boxs], [qs[1]], [qs[2]]]

    def step(stage, k):
        if 0 <= k < len(queue):
            for r in queue[k]:
                getattr(r, stage)()

    pairs = [(x_in, x), (og_in, do)]
    pairs += [(q_in.at[w], wq.at[w, pl.ds(pl.multiple_of(me * loc, 16), loc)]) for w in range(3)]
    own_rows = pl.ds(pl.multiple_of(me * loc, 16), loc)
    pairs += [(box_in, wbox.at[own_rows]), (out_in, wout.at[own_rows]), (upb_in, upb.at[me]), (up_in, wup.at[me]), (dn_in, wdn.at[me])]
    loads = [pltpu.make_async_copy(a, b, local.at[i]) for i, (a, b) in enumerate(pairs)]
    for made in loads:
        made.start()

    place.greet()
    for g in gathers:
        g.g0()

    lane = lax.broadcasted_iota(jnp.int32, (rows, 128), 1)
    sub = lax.rem(lane, 64)
    which = lax.div(sub, 16)
    freq = jnp.exp(-jnp.log(10000.0) * lax.rem(sub[:1], 16).astype(F32) / 16)
    c = coords[...].astype(F32)
    angle = jnp.where(which == 0, c[:, 0:1], jnp.where(which == 1, c[:, 1:2], jnp.where(which == 2, c[:, 2:3], c[:, 3:4]))) * freq
    f = jnp.where(lane < 64, jnp.cos(angle), jnp.sin(angle)).astype(BF16)
    feat[...] = f
    f = f.astype(F32)
    rolled = pltpu.roll(f, 64, 1)
    sin2[...] = jnp.where(lane < 64, rolled, f)
    cos2[...] = jnp.where(lane < 64, f, -rolled)
    ends = []
    total = jnp.int32(0)
    for k in range(lengths.shape[1]):
        total = total + lengths[me, k]
        ends.append(total)
    col_pos = lax.broadcasted_iota(jnp.int32, (8, rows), 1)
    col_id = sum([(col_pos >= e).astype(jnp.int32) for e in ends])[:1]
    for r in range(rows // 128):
        row_pos = lax.broadcasted_iota(jnp.int32, (128, rows), 0) + r * 128
        row_id = sum([(row_pos >= e).astype(jnp.int32) for e in ends])
        mask[r * 128:(r + 1) * 128, :] = jnp.where(row_id == col_id, 0.0, MASKED)

    def project(w, dst, first, scale):
        rs = pl.ds(pl.multiple_of(first, 128), 384)
        part = mm_t(x[...], wq[w, rs, :]).astype(BF16)
        if scale != 1.0:
            part = part * jnp.asarray(scale, BF16)
        head = lax.div(first, 128)
        for i in range(3):
            dst[head + i] = part[:, i * 128:(i + 1) * 128]

    def roll_box(first):
        rs = pl.ds(pl.multiple_of(first, 128), 384)
        boxr[rs, :] = pltpu.roll(wbox[rs, :].astype(F32), 64, 1).astype(BF16)

    def attend(pr):
        q = qp[pr]
        keys = jnp.concatenate([kp[pr], feat[...]], axis=1)
        values = vp[pr]
        rs = pl.ds(pl.multiple_of(pr * 128, 128), 128)
        box = jnp.concatenate([wbox[rs, :], boxr[rs, :]], axis=1)
        outs = []
        for h in range(2):
            qm = q * half_mask(h, BF16)
            bt = mm(qm, box)
            rot = (bt[:, :128] * sin2[...] + bt[:, 128:] * cos2[...]).astype(BF16)
            s = mm_t(jnp.concatenate([qm, rot], axis=1), keys) + mask[...]
            e = jnp.exp(s - jnp.max(s, axis=-1, keepdims=True))
            p = (e * (1.0 / jnp.sum(e, axis=-1, keepdims=True))).astype(BF16)
            prob[2 * pr + h] = p
            outs.append(mm(p, values))
        ctx[:, lanes(pr * 128)] = low_half(outs[0], outs[1]).astype(BF16)

    def at(i, steps):
        for k, run in steps.items():
            @pl.when(i == k)
            def _(run=run):
                for s in run:
                    s()

    scale = HEAD_DIM ** -0.5
    loads[0].wait()
    for w, (dst, factor) in enumerate(((qp, scale), (kp, 1.0), (vp, 1.0))):
        loads[2 + w].wait()
        gat_q[w].near()
        project(w, dst, near, factor)
        gat_q[w].g1()
    loads[5].wait()
    gat_b.near()
    gat_b.g1()
    gat_s.g1()
    roll_box(near)

    def attend_near(i, carry):
        attend(lax.div(near, 128) + i)
        at(i, {0: [gat_q[0].g2, gat_o.g1], 1: [gat_q[1].g2, gat_q[2].g2, gat_q[0].g3], 2: [gat_q[1].g3, gat_q[2].g3, gat_u.g1]})
        return carry

    lax.fori_loop(0, 3, attend_near, 0)
    gat_b.far()
    roll_box(far)
    for w, (dst, factor) in enumerate(((qp, scale), (kp, 1.0), (vp, 1.0))):
        gat_q[w].far()
        project(w, dst, far, factor)

    def attend_far(i, carry):
        attend(lax.div(far, 128) + i)
        at(i, {0: [gat_o.g2], 1: [gat_o.g3, gat_d.g1], 2: [gat_u.g2]})
        return carry

    lax.fori_loop(0, 3, attend_far, 0)
    loads[6].wait()
    gat_o.near()
    gat_o.far()

    def norm_one(r, carry):
        rs = pl.ds(pl.multiple_of(r * 256, 256), 256)
        v = mm(ctx[rs, :], wout[...]) + x[rs, :].astype(F32)
        cen = v - jnp.mean(v, axis=-1, keepdims=True)
        inv = lax.rsqrt(jnp.mean(cen * cen, axis=-1, keepdims=True) + EPSILON)
        hat = cen * inv
        hat1[rs, :] = hat
        inv1[rs, :] = jnp.broadcast_to(inv, (256, 128))
        low = (hat * n1g[...] + n1b[...]).astype(BF16)
        nl[rs, :] = low
        return carry

    lax.fori_loop(0, rows // 256, norm_one, 0)
    nlt[...] = nl[...].T

    br[...] = jnp.zeros_like(br)
    for i in (7, 8, 9):
        loads[i].wait()
    gat_s.near()
    gat_u.near()
    gat_d.near()

    def ffn(i, carry):
        at(i, {2: [gat_u.g3, gat_d.g2, gat_s.far, gat_u.far, gat_d.g3, gat_d.far]})
        jy = jnp.where(i < 2, y, 1 - y)
        jc = jnp.where(lax.rem(i, 2) == 0, place.c, 1 - place.c)
        j = jy * 2 + jc
        acts = []
        for s in range(3):
            cs = slice(s * 256, (s + 1) * 256)
            pre = mm(nl[...], wup[j, :, cs]) + upb[j, :1, cs]
            cdf = 0.5 * (1.0 + lax.erf(pre * ROOT_HALF))
            act = (pre * cdf).astype(BF16)
            slp[j, :, cs] = (cdf + pre * jnp.exp(-0.5 * pre * pre) * INV_ROOT_TAU).astype(BF16)
            actt[j, cs, :] = act.T
            acts.append(act)
        br[...] += mm(jnp.concatenate(acts, axis=1), wdn[j])
        return carry

    lax.fori_loop(0, n_tile, ffn, 0)

    small[...] = jnp.zeros_like(small)
    loads[1].wait()

    def norm_two(r, carry):
        rs = pl.ds(pl.multiple_of(r * 128, 128), 128)
        v = hat1[rs, :] * n1g[...] + n1b[...] + br[rs, :]
        cen = v - jnp.mean(v, axis=-1, keepdims=True)
        inv = lax.rsqrt(jnp.mean(cen * cen, axis=-1, keepdims=True) + EPSILON)
        hat = cen * inv
        g = do[rs, :].astype(F32)
        do[rs, :] = (hat * n2g[...] + n2b[...]).astype(BF16)
        w = g * n2g[...]
        back = inv * (w - jnp.mean(w, axis=-1, keepdims=True) - hat * jnp.mean(w * hat, axis=-1, keepdims=True))
        br[rs, :] = back
        bg[rs, :] = back.astype(BF16)
        small[0, 3:4, :] += jnp.sum(g * hat, axis=0, keepdims=True)
        small[0, 4:5, :] += jnp.sum(g, axis=0, keepdims=True)
        return carry

    lax.fori_loop(0, rows // 128, norm_two, 0)
    save_lo = pltpu.make_async_copy(do, lo, local.at[len(loads)])
    save_lo.start()

    def ffn_back(t, carry):
        s = lax.div(t, 4)
        jj = lax.rem(t, 4)
        jy = jnp.where(jj < 2, 1 - y, y)
        jc = jnp.where(lax.rem(jj, 2) == 0, 1 - place.c, place.c)
        j = jy * 2 + jc
        cs = pl.ds(pl.multiple_of(s * 256, 256), 256)
        fg = mm_t(bg[...], wdn[j, cs, :]) * slp[j, :, cs].astype(F32)
        fg = fg.astype(BF16)
        small[j, :1, cs] = jnp.sum(fg.astype(F32), axis=0, keepdims=True)
        slp[j, :, cs] = fg
        gup[j, :, cs] = mm(nlt[...], fg).astype(BF16)
        gdn[j, cs, :] = mm(actt[j, cs, :], bg[...]).astype(BF16)
        steps = {}
        for s in range(3):
            steps[4 * s] = [ups[s].s0a, dns[s].s0a]
            steps[4 * s + 2] = [ups[s].s0b, dns[s].s0b, ups[s].s1, dns[s].s1]
        at(t, steps)
        return carry

    lax.fori_loop(0, 3 * n_tile, ffn_back, 0)

    def ffn_in(j, carry):
        br[...] += mm_t(slp[j], wup[j])
        return carry

    lax.fori_loop(0, n_tile, ffn_in, 0)

    def norm_back(r, carry):
        rs = pl.ds(pl.multiple_of(r * 128, 128), 128)
        up = br[rs, :]
        hat = hat1[rs, :]
        w = up * n1g[...]
        back = inv1[rs, :1] * (w - jnp.mean(w, axis=-1, keepdims=True) - hat * jnp.mean(w * hat, axis=-1, keepdims=True))
        br[rs, :] = back
        bg[rs, :] = back.astype(BF16)
        small[0, 1:2, :] += jnp.sum(up * hat, axis=0, keepdims=True)
        small[0, 2:3, :] += jnp.sum(up, axis=0, keepdims=True)
        return carry

    lax.fori_loop(0, rows // 128, norm_back, 0)
    for j in range(1, n_tile):
        small[j, 1:5, :] = small[0, 1:5, :]
    smalls.s0a()
    smalls.s0b()
    step("s2", 0)

    for made in (gat_u.fx, gat_u.fz, gat_u.f0, gat_u.f1, gat_u.f2, gat_u.dx, gat_u.dz, gat_u.f3):
        wire.settle(made)
    save_lo.wait()
    for t in range(d // 256):
        cs = slice(t * 256, (t + 1) * 256)
        gout[cs, :] = mm(ctx[:, cs].T, bg[...]).astype(BF16)
        do[:, cs] = mm_t(bg[...], wout[cs, :]).astype(BF16)
    outr.s0a()
    outr.s0b()
    smalls.s1()
    step("s3", 0)

    def attend_back(pr):
        q8t = qp[pr].T
        up = do[:, lanes(pr * 128)]
        upt = up.T
        values = vp[pr]
        keys = jnp.concatenate([kp[pr], feat[...]], axis=1)
        rs = pl.ds(pl.multiple_of(pr * 128, 128), 128)
        box = wbox[rs, :]
        dots = up.astype(F32) * ctx[:, lanes(pr * 128)].astype(F32)
        dqs, dks, dvs = [], [], []
        for h in range(2):
            hs = slice(64 * h, 64 * h + 64)
            p = prob[2 * pr + h]
            dot = jnp.sum(dots * half_mask(h, F32), axis=-1, keepdims=True)
            ds = (p.astype(F32) * (mm_t(up * half_mask(h, BF16), values) - dot)).astype(BF16)
            dvs.append(mm(upt[hs], p))
            dks.append(mm(q8t[hs], ds))
            da = mm(ds, keys) * (HEAD_DIM ** -0.5)
            rg = da[:, 128:]
            turn = (rg * sin2[...] - pltpu.roll(rg, 64, 1) * cos2[...]).astype(BF16)
            gbox[pl.ds(pl.multiple_of(pr * 128 + 64 * h, 64), 64), :] = (mm(q8t[hs], turn) * (HEAD_DIM ** 0.5)).astype(BF16)
            dqs.append(da[:, :128] + mm_t(turn, box))
        dq = low_half(dqs[0], dqs[1]).astype(BF16)
        dkt = jnp.concatenate(dks, axis=0).astype(BF16)
        dvt = jnp.concatenate(dvs, axis=0).astype(BF16)
        dt[0, rs, :] = dq.T
        dt[1, rs, :] = dkt
        dt[2, rs, :] = dvt
        qp[pr] = dq
        kp[pr] = dkt.T
        vp[pr] = dvt.T

    def weight_grads(first):
        rs = pl.ds(pl.multiple_of(first, 128), 384)
        for w in range(3):
            gq[w, rs, :] = mm(dt[w, rs, :], x[...]).astype(BF16)

    def attend_back_far(i, carry):
        attend_back(lax.div(far, 128) + i)
        at(i, {0: [outr.s1]})
        return carry

    lax.fori_loop(0, 3, attend_back_far, 0)
    weight_grads(far)
    for r in qs + [boxs]:
        r.s0a()
    step("s2", 1)
    step("s4", 0)

    def attend_back_near(i, carry):
        attend_back(lax.div(near, 128) + i)
        at(i, {0: [qs[0].s1, qs[1].s1, qs[2].s1, boxs.s1], 1: [lambda: step("s3", 1)], 2: [lambda: step("s2", 2), lambda: step("s5", 0)]})
        return carry

    lax.fori_loop(0, 3, attend_back_near, 0)
    weight_grads(near)
    for r in qs + [boxs]:
        r.s0b()
    step("s4", 1)

    for r in range(rows // 256):
        rs = slice(r * 256, (r + 1) * 256)
        acc = br[rs, :]
        for w, src in enumerate((qp, kp, vp)):
            whole = jnp.concatenate([src[i, rs] for i in range(d // 128)], axis=1)
            acc += mm(whole, wq[w])
        br[rs, :] = acc
    save_ig = pltpu.make_async_copy(br, ig, local.at[len(loads) + 1])
    save_ig.start()
    step("s3", 2)
    step("s6", 0)

    for k in range(3, len(queue) + 2):
        step("s2", k)
        step("s5", k - 2)
        step("s4", k - 1)
        step("s3", k)
        step("s6", k - 2)

    ends = [(ry_up, gup_out), (ry_dn, gdn_out), (ry_o, gout_out), (ry_b, gbox_out), (small.at[me], small_out), (ry_q, gq_out)]
    saves = [pltpu.make_async_copy(a, b, local.at[len(loads) + 2 + i]) for i, (a, b) in enumerate(ends)]
    for made in saves:
        made.start()
    wire.drain()
    for made in saves:
        made.wait()
    save_ig.wait()


def on_device(hidden_in, box_coords, page_lengths, qkv_weight, box_weight, out_weight, norm1_gain, norm1_bias,
              up_weight, up_bias, down_weight, norm2_gain, norm2_bias, out_grad):
    rows, d = hidden_in.shape
    n = lax.axis_size("mp")
    loc = qkv_weight.shape[2]
    f = up_weight.shape[1]
    vm = pl.BlockSpec(memory_space=pltpu.VMEM)
    sm = pl.BlockSpec(memory_space=pltpu.SMEM)
    hb = pl.BlockSpec(memory_space=pl.ANY)
    S = jax.ShapeDtypeStruct
    V = pltpu.VMEM
    np_ = d // 128
    D = pltpu.SemaphoreType.DMA
    outs = pl.pallas_call(
        kernel,
        out_shape=[S((rows, d), BF16), S((rows, d), F32), S((3, loc, d), BF16), S((loc, 128), BF16), S((loc, d), BF16),
                   S((d, f), BF16), S((f, d), BF16), S((8, d), F32)],
        in_specs=[hb, vm, sm] + [hb] * 7 + [vm] * 4,
        out_specs=[hb] * 8,
        scratch_shapes=[
            V((rows, d), BF16), V((3, d, d), BF16), V((d, 128), BF16), V((d, d), BF16), V((n, d, f), BF16),
            V((n, 8, d), F32), V((n, f, d), BF16), V((d, 128), BF16), V((n, d, f), BF16), V((n, f, d), BF16), V((n, 8, d), F32),
            V((rows, 128), BF16), V((rows, 128), F32), V((rows, 128), F32), V((rows, rows), F32),
            V((np_, rows, 128), BF16), V((np_, rows, 128), BF16), V((np_, rows, 128), BF16),
            V((d // 64, rows, rows), BF16), V((rows, d), BF16), V((rows, d), F32), V((rows, 128), F32),
            V((rows, d), BF16), V((d, rows), BF16), V((n, f, rows), BF16), V((n, rows, f), BF16),
            V((rows, d), F32), V((rows, d), BF16), V((d, 128), BF16), V((rows, d), BF16),
            V((2, d, f), BF16), V((2, f, d), BF16), V((d, f), BF16), V((f, d), BF16), V((3, d, 128), BF16), V((3, 256, d // 2), BF16),
            V((3, 3, d // 4, 128), BF16), V((3, 3, 64, d // 2), BF16),
            V((2, 3, loc, d), BF16), V((3, loc, d), BF16), V((3, loc, d // 2), BF16), V((3, 3, loc // 4, d // 2), BF16),
            V((2, loc, d), BF16), V((loc, d), BF16), V((loc, d // 2), BF16), V((3, loc // 4, d // 2), BF16),
            V((2, loc, 128), BF16), V((loc, 128), BF16), V((loc, 128), BF16), V((3, loc // 4, 128), BF16),
            V((2, 8, d), F32), V((8, d), F32), V((8, d), F32), V((4, 8, d), F32),
            D((N_COPY,)), D((N_COPY,)), D((24,)),
        ],
        compiler_params=pltpu.CompilerParams(vmem_limit_bytes=67_000_000, collective_id=0, has_side_effects=True),
        name="layer",
    )(hidden_in, box_coords, page_lengths, out_grad, jnp.transpose(qkv_weight, (1, 2, 0)), box_weight.T, out_weight, up_weight,
      jnp.broadcast_to(up_bias.astype(F32)[None], (8, up_bias.shape[0])), down_weight,
      norm1_gain[None], norm1_bias[None], norm2_gain[None], norm2_bias[None])
    lo, ig, gq, gbox, gout, gup, gdn, small = outs
    n_dp = lax.axis_size("dp")
    if n_dp > 8:
        groups = [[g * 8 + i for g in range(n_dp // 8)] for i in range(8)]
        gq, gbox, gout, gup, gdn, small = [
            lax.psum(v.astype(F32), "dp", axis_index_groups=groups) for v in (gq, gbox, gout, gup, gdn, small)]
    up = lambda v: v.astype(F32)
    return (lo, ig, jnp.transpose(up(gq), (2, 0, 1)), up(gbox).T, up(gout), small[1], small[2], up(gup), small[0], up(gdn), small[3], small[4])


def solution(mesh):
    rows = P(("dp", "mp"), None)
    in_specs = (rows, rows, P("dp", None), P(None, None, "mp"), P(None, "mp"), P("mp", None), P(), P(),
                P(None, "mp"), P("mp"), P("mp", None), P(), P(), rows)
    out_specs = (rows, rows, P(None, None, "mp"), P(None, "mp"), P("mp", None), P(), P(),
                 P(None, "mp"), P("mp"), P("mp", None), P(), P())
    return jax.shard_map(on_device, mesh=mesh, in_specs=in_specs, out_specs=out_specs, check_vma=False)
```
